32 devices in a mesh: replica: 8 (over y, x, core), fsdp: 4 (over z).
Axes of the slice: x: 2, y: 2, z: 4, core: 2. Of those that a mesh axis runs over, the one named last changes fastest.
Arguments:
- momentum: bfloat16 [8, 4, 384, 1024], P('replica', None, 'fsdp'), may hold values from -400 to 400
- weights: bfloat16 [8, 4, 384, 1024], P('replica', 'fsdp'), may hold values from -6 to 6
- tokens: bfloat16 [8, 1024, 1024], P('replica', 'fsdp'), may hold values from -6 to 6
- routes: int32 [8, 1024, 1], P('replica', 'fsdp'), may hold values from 0 to 3; in each aligned block of 256 rows (0 to 255, 256 to 511, ..., all dimensions but the last counted through in order) at most 128 rows name the same one
Outputs:
- new_weight: bfloat16 [8, 4, 384, 1024], P('replica', 'fsdp')
- expert_rows: bfloat16 [8, 4, 512, 384], P('replica', 'fsdp')
The draws below stay inside these ranges and needn't reach their ends.
Inputs may be any that keep to these rules, and one draw needn't show every extreme that they name: `routes`: within one replica, the 256 rows of one device name each expert at most 128 times, a bound that some block reaches.
All inputs are finite; a program needn't handle non-finite values.
Results may differ from the reference program's by a relative error of at most 0.008.
Values may be sent and summed in bfloat16 or wider, within the bound.
No kernel may reach another device: no remote copies, remote signals or barrier semaphores. Data moves between devices by JAX's collectives and lax.ppermute only.
A program may use at most 64 MiB of HBM per device.

```python
import math
import jax
import jax.numpy as jnp
import numpy as np
from jax import lax

D = 1024
FF = 384
TOK_DEV = 256
ITERS = 2
GOSSIP_BIT = 2
R = 8
EXPERTS = 4
CAP = 128
SLOTS = 512
TOKENS = 1024
N_FSDP = 4


def draw_momentum(key, part):
    keys = jax.random.split(key, 3)
    shape = (R, EXPERTS, FF, D)
    base = jax.random.truncated_normal(keys[0], -4.0, 4.0, shape, jnp.float32)
    row_scale = jnp.exp(jax.random.uniform(keys[1], (R, EXPERTS, FF, 1), jnp.float32, 0.0, math.log(10.0)))
    col_scale = jnp.exp(jax.random.uniform(keys[2], (R, EXPERTS, 1, D), jnp.float32, 0.0, math.log(10.0)))
    values = base * row_scale * col_scale
    return values.astype(jnp.bfloat16)


def block_levels(own_key, extent, cuts, low, largest):
    factor_of, own = 1.0, jax.random.fold_in(own_key, 6)
    for axis_at, blocks in cuts:
        steps = jnp.exp(jax.random.uniform(jax.random.fold_in(own, axis_at), (blocks,), jnp.float32, low / len(cuts), largest / len(cuts)))
        factor_of = factor_of * jnp.repeat(steps, extent[axis_at] // blocks).reshape([-1 if axis == axis_at else 1 for axis in range(len(extent))])
    return factor_of


def routed_block(stream_key, own, number, rows, amount, top, most, skew):
    order = jax.random.permutation(stream_key, amount)
    heavy_load, ordinary = portions_of(amount, rows * top, most, skew, True), portions_of(amount, rows * top, most, skew, False)
    places = jnp.arange(amount)

    def named(sizes, rotation):
        used = int((sizes > 0).sum())
        fixed = max(1, used // 4)
        moved = fixed + (places - fixed + rotation * (used - fixed)) % max(1, amount - fixed)
        return jnp.zeros((amount,), jnp.int32).at[order[jnp.where(places < fixed, places, moved)]].set(jnp.asarray(sizes, jnp.int32))

    sizes = jnp.where(number % 4 == 0, named(heavy_load, number // 4), named(ordinary, number - number // 4 - 1))
    mixed = jax.random.permutation(jax.random.fold_in(own, 3), amount)
    giver, receiver = mixed[0:amount // 2 * 2:2], mixed[1:amount // 2 * 2:2]
    margin = jnp.minimum(sizes[giver] - 1, most - sizes[receiver]) // 2
    margin = jnp.where((giver == order[0]) | (receiver == order[0]) | (sizes[receiver] == 0), 0, jnp.maximum(margin, 0))
    moved = jax.random.randint(jax.random.fold_in(own, 4), (amount // 2,), 0, 1 << 20) % (margin + 1)
    sizes = sizes.at[giver].add(-moved).at[receiver].add(moved)
    members = jnp.searchsorted(jnp.cumsum(sizes), jnp.arange(rows * top), side="right").astype(jnp.int32)
    grid = members.reshape(top, rows).T
    grid = grid[jax.random.permutation(jax.random.fold_in(own, 1), rows)]
    rotation = jax.random.randint(jax.random.fold_in(own, 2), (rows, 1), 0, top)
    return jnp.take_along_axis(grid, (jnp.arange(top)[None, :] + rotation) % top, axis=1)


def portions_of(number_of, total, reach, skew, full):
    loads = [(1 << 20) // math.isqrt(rank ** skew) + 1 for rank in range(1, number_of + 1)]
    largest = reach if full else min(reach, max(-(-total // number_of), total * loads[0] // sum(loads)))
    least = 1 if total - largest >= number_of - 1 else 0
    given, rest = [largest] + [least] * (number_of - 1), total - largest - least * (number_of - 1)
    while rest > 0:
        movable = [i for i in range(1, number_of) if given[i] < largest] or [i for i in range(1, number_of) if given[i] < reach]
        mass, budget = sum([loads[i] for i in movable]), rest
        for i in movable:
            addition = min(reach - given[i], max(1, budget * loads[i] // mass), rest)
            given[i] = given[i] + addition
            rest = rest - addition
    return np.array(given)


def scatter_about(own_key, extent, deviation, bound, shards=(), kind=jnp.bfloat16):
    drawn = jax.random.normal(own_key, extent, jnp.float32) * deviation
    if len(shards) > 0:
        drawn = block_levels(own_key, extent, shards, -0.22, 0.18) * drawn
    return jnp.clip(drawn, min=-bound, max=bound).astype(kind)


def setup_inputs(seed: int = 0) -> dict:
    seeds = jax.random.split(jax.random.key(seed), 5)
    momentum = draw_momentum(jax.random.fold_in(seeds[4], 71), 0)
    weights = scatter_about(seeds[1], (R, EXPERTS, FF, D), 1.0, 6.0, ((0, 8), (1, 4)))
    tokens = scatter_about(seeds[2], (R, TOKENS, D), 1.0, 6.0, ((0, 8), (1, 4)))
    routes_keys = jax.random.split(jax.random.fold_in(seeds[3], 1), R * TOKENS // TOK_DEV)
    routes_turns = jax.random.permutation(jax.random.fold_in(seeds[3], 3), R * TOKENS // TOK_DEV)
    routes = jax.vmap(lambda own, number: routed_block(jax.random.fold_in(seeds[3], 2), own, number, TOK_DEV, EXPERTS, 1, CAP, 2))(routes_keys, routes_turns).reshape((R, TOKENS, 1))
    return {"momentum": momentum, "weights": weights, "tokens": tokens, "routes": routes}


coef_a = 3.4445
coef_b = -4.775
coef_c = 2.0315
step_rate = 0.5

def orthogonalize(matrix):
    values = matrix.astype(jnp.float32)
    ortho = (values / (jnp.sqrt(jnp.sum(values * values)) + 1e-07)).astype(jnp.bfloat16)
    for step in range(ITERS):
        gram = jnp.dot(ortho, ortho.T, preferred_element_type=jnp.float32).astype(jnp.bfloat16)
        poly = (coef_b * gram.astype(jnp.float32) + coef_c * jnp.dot(gram, gram, preferred_element_type=jnp.float32)).astype(jnp.bfloat16)
        ortho = (coef_a * ortho.astype(jnp.float32) + jnp.dot(poly, ortho, preferred_element_type=jnp.float32)).astype(jnp.bfloat16)
    return ortho

def update_one(pair):
    matrix, weight = pair
    ortho = orthogonalize(matrix)
    return (weight.astype(jnp.float32) - step_rate * math.sqrt(D) * ortho.astype(jnp.float32)).astype(jnp.bfloat16)

def reference(momentum, weights, tokens, routes):
    flat_mom = momentum.reshape(R * EXPERTS, FF, D)
    flat_w = weights.reshape(R * EXPERTS, FF, D)
    updated = lax.map(update_one, (flat_mom, flat_w)).reshape(R, EXPERTS, FF, D)
    partner_idx = jnp.bitwise_xor(jnp.arange(R, dtype=jnp.int32), jnp.int32(2 ** GOSSIP_BIT))
    new_weight = (0.5 * (updated.astype(jnp.float32) + updated[partner_idx].astype(jnp.float32))).astype(jnp.bfloat16)
    expert_id = routes[:, :, 0]
    onehot = (expert_id[:, :, None] == jnp.arange(EXPERTS, dtype=jnp.int32)[None, None, :]).astype(jnp.int32)
    blocks = onehot.reshape(R, N_FSDP, TOK_DEV, EXPERTS)
    position = lax.optimization_barrier(jnp.sum((jnp.cumsum(blocks, axis=2) - 1) * blocks, axis=3))
    source = jnp.arange(N_FSDP, dtype=jnp.int32)[None, :, None]
    slot_id = (expert_id.reshape(R, N_FSDP, TOK_DEV) * SLOTS + source * CAP + position).reshape(R, TOKENS).astype(jnp.int32)

    def project(item):
        tok, slot, weight = item
        slotted = jnp.zeros((EXPERTS * SLOTS, D), jnp.bfloat16).at[slot].set(tok)
        slotted = slotted.reshape(EXPERTS, SLOTS, D)
        rows = jnp.einsum('esd,efd->esf', slotted.astype(jnp.float32), weight.astype(jnp.float32))
        return (rows / math.sqrt(D)).astype(jnp.bfloat16)
    expert_rows = lax.map(project, (tokens, slot_id, new_weight))
    return (new_weight, expert_rows)
```

```python
import functools
import math

import jax
import jax.numpy as jnp
from jax import lax
from jax.experimental import pallas as pl
from jax.experimental.pallas import tpu as pltpu
from jax.sharding import PartitionSpec as P

ITERS = 2
GOSSIP_BIT = 2


coef_a = 3.4445
coef_b = -4.775
coef_c = 2.0315
step_rate = 0.5

VMEM = pl.BlockSpec(memory_space=pltpu.VMEM)
SMEM = pl.BlockSpec(memory_space=pltpu.SMEM)


def dot(a, b):
    return jnp.dot(a, b, preferred_element_type=jnp.float32)


def dot_t(a, b):
    return lax.dot_general(a, b, (((1,), (1,)), ((), ())), preferred_element_type=jnp.float32)


def other(me, hop, nodes):
    if nodes & (nodes - 1) == 0:
        return me ^ hop
    return lax.rem(hop - me + nodes, nodes)


def trade(block, hop, nodes):
    if nodes & (nodes - 1) == 0:
        pairs = [(i, i ^ hop) for i in range(nodes)]
    else:
        pairs = [(i, (hop - i) % nodes) for i in range(nodes)]
    return lax.ppermute(block, "fsdp", pairs)


def update_kernel(nodes, width, place_ref, *refs):
    blocks, weight_ref, out_ref, x_ref = refs[:nodes], refs[nodes], refs[nodes + 1], refs[nodes + 2]
    rows = blocks[0].shape[0]
    total = nodes * rows
    for k in range(nodes):
        x_ref[k * rows : (k + 1) * rows, :] = blocks[k][...]
    x = x_ref[...]
    gram = dot_t(x, x)
    on_diagonal = lax.broadcasted_iota(jnp.int32, (total, total), 0) == lax.broadcasted_iota(
        jnp.int32, (total, total), 1
    )
    square = jnp.sum(jnp.where(on_diagonal, gram, 0.0))
    scale = 1.0 / (jnp.sqrt(jnp.full((1, 1), square, jnp.float32)) + 1e-07)
    gram = gram * scale * scale
    keep, mix = 1.0, None
    now = gram
    for step in range(ITERS):
        low = now.astype(jnp.bfloat16)
        poly = coef_b * now + coef_c * dot(low, low)
        poly_low = poly.astype(jnp.bfloat16)
        if step + 1 < ITERS:
            first = dot(poly_low, low)
            second = dot(poly_low, first.astype(jnp.bfloat16))
            now = coef_a * coef_a * now + 2.0 * coef_a * first + second
        if mix is None:
            mix = keep * poly
        else:
            mix = coef_a * mix + keep * poly + dot(poly_low, mix.astype(jnp.bfloat16))
        keep = keep * coef_a
    mix = (mix * scale).astype(jnp.bfloat16)
    rate = step_rate * math.sqrt(width)
    for k in range(nodes):
        change = dot(mix[k * rows : (k + 1) * rows, :], x) + (keep * scale) * blocks[k][...].astype(
            jnp.float32
        )
        at = pl.ds(pl.multiple_of(place_ref[k] * rows, rows), rows)
        out_ref[at, :] = (weight_ref[at, :].astype(jnp.float32) - rate * change).astype(jnp.bfloat16)


def project_kernel(nodes, width, place_ref, *refs):
    blocks, own_ref, partner_ref = refs[:nodes], refs[nodes], refs[nodes + 1]
    weight_ref, rows_ref, slot_ref = refs[nodes + 2], refs[nodes + 3], refs[nodes + 4]
    capacity = blocks[0].shape[0]
    weight = (
        0.5 * (own_ref[...].astype(jnp.float32) + partner_ref[...].astype(jnp.float32))
    ).astype(jnp.bfloat16)
    weight_ref[...] = weight
    for k in range(nodes):
        at = pl.ds(pl.multiple_of(place_ref[k] * capacity, capacity), capacity)
        slot_ref[at, :] = blocks[k][...]
    rows_ref[...] = (dot_t(slot_ref[...], weight) * (1.0 / math.sqrt(width))).astype(jnp.bfloat16)


def per_device(momentum, weights, tokens, routes):
    nodes = lax.axis_size("fsdp")
    me = lax.axis_index("fsdp")
    rows, width = momentum.shape[2], momentum.shape[3]
    total = weights.shape[2]
    experts = momentum.shape[1]
    tok_rows = tokens.shape[1]
    capacity = 2 * tok_rows // nodes
    hops = range(1, nodes)
    place = jnp.stack([other(me, k, nodes) for k in range(nodes)]).astype(jnp.int32)

    shards = [lax.dynamic_index_in_dim(momentum[0], place[k], 0, False) for k in range(nodes)]
    blocks = [shards[0]] + [trade(shards[k], k, nodes) for k in hops]

    expert_id = routes[0, :, 0]
    onehot = (expert_id[:, None] == jnp.arange(experts, dtype=jnp.int32)[None, :]).astype(jnp.int32)
    position = jnp.sum((jnp.cumsum(onehot, axis=0) - 1) * onehot, axis=1)
    packed = []
    for k in range(nodes):
        wanted = jnp.where(expert_id == place[k], position, -1)
        placing = (wanted[None, :] == jnp.arange(capacity, dtype=jnp.int32)[:, None]).astype(
            jnp.bfloat16
        )
        packed.append(dot(placing, tokens[0]).astype(jnp.bfloat16))
    slots = [packed[0]] + [trade(packed[k], k, nodes) for k in hops]

    updated = pl.pallas_call(
        functools.partial(update_kernel, nodes, width),
        out_shape=jax.ShapeDtypeStruct((total, width), jnp.bfloat16),
        in_specs=[SMEM] + [VMEM] * (nodes + 1),
        out_specs=VMEM,
        scratch_shapes=[pltpu.VMEM((total, width), jnp.bfloat16)],
        compiler_params=pltpu.CompilerParams(vmem_limit_bytes=24 << 20),
        cost_estimate=pl.CostEstimate(
            flops=4 * total * total * width + 10 * total**3,
            bytes_accessed=6 * total * width,
            transcendentals=0,
        ),
        name="update",
    )(place, *blocks, weights[0, 0])
    partner = lax.ppermute(
        updated, "replica", [(i, i ^ 1 << GOSSIP_BIT) for i in range(lax.axis_size("replica"))]
    )
    averaged, expert_rows = pl.pallas_call(
        functools.partial(project_kernel, nodes, width),
        out_shape=(
            jax.ShapeDtypeStruct((total, width), jnp.bfloat16),
            jax.ShapeDtypeStruct((nodes * capacity, total), jnp.bfloat16),
        ),
        in_specs=[SMEM] + [VMEM] * (nodes + 2),
        out_specs=(VMEM, VMEM),
        scratch_shapes=[pltpu.VMEM((nodes * capacity, width), jnp.bfloat16)],
        compiler_params=pltpu.CompilerParams(vmem_limit_bytes=24 << 20),
        cost_estimate=pl.CostEstimate(
            flops=2 * nodes * capacity * width * total,
            bytes_accessed=6 * total * width + 2 * nodes * capacity * (width + total),
            transcendentals=0,
        ),
        name="project",
    )(place, *slots, updated, partner)
    return (averaged[None, None], expert_rows[None, None])


def solution(mesh):
    in_specs = (
        P("replica", None, "fsdp", None),
        P("replica", "fsdp", None, None),
        P("replica", "fsdp", None),
        P("replica", "fsdp", None),
    )
    out_specs = (P("replica", "fsdp", None, None), P("replica", "fsdp", None, None))
    return jax.shard_map(
        per_device, mesh=mesh, in_specs=in_specs, out_specs=out_specs, check_vma=False
    )
```

```python
import functools
import math

import jax
import jax.numpy as jnp
from jax import lax
from jax.experimental import pallas as pl
from jax.experimental.pallas import tpu as pltpu
from jax.sharding import PartitionSpec as P


ITERS = 2
GOSSIP_BIT = 2


coef_a = 3.4445
coef_b = -4.775
coef_c = 2.0315
step_rate = 0.5

VMEM = pl.BlockSpec(memory_space=pltpu.VMEM)
SMEM = pl.BlockSpec(memory_space=pltpu.SMEM)


def dot(a, b):
    return jnp.dot(a, b, preferred_element_type=jnp.float32)


def dot_t(a, b):
    return lax.dot_general(a, b, (((1,), (1,)), ((), ())), preferred_element_type=jnp.float32)


def other(me, hop, nodes):
    if nodes & (nodes - 1) == 0:
        return me ^ hop
    return lax.rem(hop - me + nodes, nodes)


def far_first(nodes):
    return (*range(2, nodes), 1) if nodes > 1 else ()


def trade(block, hop, nodes):
    if nodes & (nodes - 1) == 0:
        pairs = [(i, i ^ hop) for i in range(nodes)]
    else:
        pairs = [(i, (hop - i) % nodes) for i in range(nodes)]
    return lax.ppermute(block, "fsdp", pairs)


def pack_kernel(nodes, capacity, place_ref, routes_ref, tokens_ref, *out_refs):
    tok_rows = routes_ref.shape[1]
    routes = routes_ref[...]
    earlier = lax.broadcasted_iota(jnp.int32, (tok_rows, tok_rows), 0) < lax.broadcasted_iota(
        jnp.int32, (tok_rows, tok_rows), 1
    )
    earlier = jnp.where(earlier, 1.0, 0.0).astype(jnp.bfloat16)
    slot = lax.broadcasted_iota(jnp.int32, (capacity, tok_rows), 0)
    tokens = tokens_ref[...]
    for k in range(nodes):
        here = routes == place_ref[k]
        count = dot(jnp.where(here, 1.0, 0.0).astype(jnp.bfloat16), earlier)
        position = jnp.where(here, count.astype(jnp.int32), -1)
        placing = jnp.where(slot == position, 1.0, 0.0).astype(jnp.bfloat16)
        out_refs[k][...] = dot(placing, tokens).astype(jnp.bfloat16)


def update_kernel(nodes, width, place_ref, *refs):
    blocks, weight_ref, out_ref, x_ref = refs[:nodes], refs[nodes], refs[nodes + 1], refs[nodes + 2]
    rows = blocks[0].shape[0]
    total = nodes * rows
    for k in range(nodes):
        x_ref[k * rows : (k + 1) * rows, :] = blocks[k][...]
    x = x_ref[...]
    gram = dot_t(x, x)
    on_diagonal = lax.broadcasted_iota(jnp.int32, (total, total), 0) == lax.broadcasted_iota(
        jnp.int32, (total, total), 1
    )
    square = jnp.sum(jnp.where(on_diagonal, gram, 0.0))
    scale = 1.0 / (jnp.sqrt(jnp.full((1, 1), square, jnp.float32)) + 1e-07)
    gram = gram * scale * scale
    keep, mix = 1.0, None
    now = gram
    for step in range(ITERS):
        low = now.astype(jnp.bfloat16)
        poly = coef_b * now + coef_c * dot(low, low)
        poly_low = poly.astype(jnp.bfloat16)
        if step + 1 < ITERS:
            first = dot(poly_low, low)
            second = dot(poly_low, first.astype(jnp.bfloat16))
            now = coef_a * coef_a * now + 2.0 * coef_a * first + second
        if mix is None:
            mix = keep * poly
        else:
            mix = coef_a * mix + keep * poly + dot(poly_low, mix.astype(jnp.bfloat16))
        keep = keep * coef_a
    mix = (mix * scale).astype(jnp.bfloat16)
    rate = step_rate * math.sqrt(width)
    for k in range(nodes):
        change = dot(mix[k * rows : (k + 1) * rows, :], x) + (keep * scale) * blocks[k][...].astype(
            jnp.float32
        )
        at = pl.ds(pl.multiple_of(place_ref[k] * rows, rows), rows)
        out_ref[at, :] = (weight_ref[at, :].astype(jnp.float32) - rate * change).astype(jnp.bfloat16)


def project_kernel(nodes, width, place_ref, *refs):
    blocks, own_ref, partner_ref = refs[:nodes], refs[nodes], refs[nodes + 1]
    weight_ref, rows_ref, slot_ref = refs[nodes + 2], refs[nodes + 3], refs[nodes + 4]
    capacity = blocks[0].shape[0]
    weight = (
        0.5 * (own_ref[...].astype(jnp.float32) + partner_ref[...].astype(jnp.float32))
    ).astype(jnp.bfloat16)
    weight_ref[...] = weight
    for k in range(nodes):
        at = pl.ds(pl.multiple_of(place_ref[k] * capacity, capacity), capacity)
        slot_ref[at, :] = blocks[k][...]
    rows_ref[...] = (dot_t(slot_ref[...], weight) * (1.0 / math.sqrt(width))).astype(jnp.bfloat16)


def per_device(momentum, weights, tokens, routes):
    nodes = lax.axis_size("fsdp")
    me = lax.axis_index("fsdp")
    width = momentum.shape[3]
    total = weights.shape[2]
    tok_rows = tokens.shape[1]
    capacity = 2 * tok_rows // nodes
    hops = range(1, nodes)
    place = jnp.stack([other(me, k, nodes) for k in range(nodes)]).astype(jnp.int32)

    shards = [lax.dynamic_index_in_dim(momentum[0], place[k], 0, False) for k in range(nodes)]
    blocks = {0: shards[0]}
    for k in far_first(nodes):
        blocks[k] = trade(shards[k], k, nodes)

    packed = list(
        pl.pallas_call(
            functools.partial(pack_kernel, nodes, capacity),
            out_shape=[jax.ShapeDtypeStruct((capacity, width), jnp.bfloat16)] * nodes,
            in_specs=[SMEM, VMEM, VMEM],
            out_specs=[VMEM] * nodes,
            compiler_params=pltpu.CompilerParams(vmem_limit_bytes=16 << 20),
            cost_estimate=pl.CostEstimate(
                flops=2 * nodes * capacity * tok_rows * width,
                bytes_accessed=2 * (tok_rows + nodes * capacity) * width,
                transcendentals=0,
            ),
            name="pack",
        )(place, routes.reshape(1, tok_rows), tokens[0])
    )
    slots = {0: packed[0]}
    for k in hops:
        slots[k] = trade(packed[k], k, nodes)
    blocks = [blocks[k] for k in range(nodes)]
    slots = [slots[k] for k in range(nodes)]

    updated = pl.pallas_call(
        functools.partial(update_kernel, nodes, width),
        out_shape=jax.ShapeDtypeStruct((total, width), jnp.bfloat16),
        in_specs=[SMEM] + [VMEM] * (nodes + 1),
        out_specs=VMEM,
        scratch_shapes=[pltpu.VMEM((total, width), jnp.bfloat16)],
        compiler_params=pltpu.CompilerParams(vmem_limit_bytes=24 << 20),
        cost_estimate=pl.CostEstimate(
            flops=4 * total * total * width + 10 * total**3,
            bytes_accessed=6 * total * width,
            transcendentals=0,
        ),
        name="update",
    )(place, *blocks, weights[0, 0])
    partner = lax.ppermute(
        updated, "replica", [(i, i ^ 1 << GOSSIP_BIT) for i in range(lax.axis_size("replica"))]
    )
    averaged, expert_rows = pl.pallas_call(
        functools.partial(project_kernel, nodes, width),
        out_shape=(
            jax.ShapeDtypeStruct((total, width), jnp.bfloat16),
            jax.ShapeDtypeStruct((nodes * capacity, total), jnp.bfloat16),
        ),
        in_specs=[SMEM] + [VMEM] * (nodes + 2),
        out_specs=(VMEM, VMEM),
        scratch_shapes=[pltpu.VMEM((nodes * capacity, width), jnp.bfloat16)],
        compiler_params=pltpu.CompilerParams(vmem_limit_bytes=24 << 20),
        cost_estimate=pl.CostEstimate(
            flops=2 * nodes * capacity * width * total,
            bytes_accessed=6 * total * width + 2 * nodes * capacity * (width + total),
            transcendentals=0,
        ),
        name="project",
    )(place, *slots, updated, partner)
    return (averaged[None, None], expert_rows[None, None])


def solution(mesh):
    in_specs = (
        P("replica", None, "fsdp", None),
        P("replica", "fsdp", None, None),
        P("replica", "fsdp", None),
        P("replica", "fsdp", None),
    )
    out_specs = (P("replica", "fsdp", None, None), P("replica", "fsdp", None, None))

    return jax.shard_map(per_device, mesh=mesh, in_specs=in_specs, out_specs=out_specs, check_vma=False)
```

```python
import functools
import math

import jax
import jax.numpy as jnp
from jax import lax
from jax.experimental import pallas as pl
from jax.experimental.pallas import tpu as pltpu
from jax.sharding import PartitionSpec as P


ITERS = 2
GOSSIP_BIT = 2


coef_a = 3.4445
coef_b = -4.775
coef_c = 2.0315
step_rate = 0.5
MH = (2, 3, 1)
TH = (1, 2, 3)
STEPS = {
    1: (1, 0, 3, 2),
    2: (2, 3, 0, 1),
    3: (3, 2, 1, 0),
    "a1": (1, 2, 3, 0),
    "a3": (3, 0, 1, 2),
    "b1": (1, 3, 0, 2),
    "b3": (2, 0, 3, 1),
    "c1": (2, 3, 1, 0),
    "c3": (3, 2, 0, 1),
}

VMEM = pl.BlockSpec(memory_space=pltpu.VMEM)


def dot(a, b):
    return jnp.dot(a, b, preferred_element_type=jnp.float32)


def dot_t(a, b):
    return lax.dot_general(a, b, (((1,), (1,)), ((), ())), preferred_element_type=jnp.float32)


def steps(nodes, order):
    if nodes == 4:
        return [STEPS[k] for k in order]
    if nodes & (nodes - 1) == 0:
        return [tuple(i ^ k for i in range(nodes)) for k in (*range(2, nodes), 1)]
    return [tuple((i + k) % nodes for i in range(nodes)) for k in (*range(2, nodes), 1)]


def inverse(step):
    return tuple(step.index(i) for i in range(len(step)))


def at(step, me):
    hop = step[0]
    if all(to == i ^ hop for i, to in enumerate(step)):
        return me ^ hop
    found = step[0]
    for i, to in enumerate(step[1:], 1):
        found = jnp.where(me == i, to, found)
    return found


def trade(block, step):
    return lax.ppermute(block, "fsdp", list(enumerate(step)))


def slice_kernel(step, source_ref, out_ref, sem):
    cp = pltpu.make_async_copy(source_ref.at[at(step, lax.axis_index("fsdp"))], out_ref, sem)
    cp.start()
    cp.wait()


def pack_kernel(to, capacity, routes_ref, tokens_ref, *out_refs):
    tok_rows = routes_ref.shape[1]
    routes = routes_ref[...]
    me = lax.axis_index("fsdp")
    earlier = lax.broadcasted_iota(jnp.int32, (tok_rows, tok_rows), 0) < lax.broadcasted_iota(
        jnp.int32, (tok_rows, tok_rows), 1
    )
    earlier = jnp.where(earlier, 1.0, 0.0).astype(jnp.bfloat16)
    slot = lax.broadcasted_iota(jnp.int32, (capacity, tok_rows), 0)
    tokens = tokens_ref[...]
    for k, step in enumerate(to):
        here = routes == at(step, me)
        count = dot(jnp.where(here, 1.0, 0.0).astype(jnp.bfloat16), earlier)
        position = jnp.where(here, count.astype(jnp.int32), -1)
        placing = jnp.where(slot == position, 1.0, 0.0).astype(jnp.bfloat16)
        out_refs[k][...] = dot(placing, tokens).astype(jnp.bfloat16)


def row_parts(rows):
    part = 128 if rows % 128 == 0 else rows
    return [slice(i, i + part) for i in range(0, rows, part)]


def update_kernel(come, width, *refs):
    nodes = len(come)
    blocks, weight_ref, out_ref, x_ref = refs[:nodes], refs[nodes], refs[nodes + 1], refs[nodes + 2]
    me = lax.axis_index("fsdp")
    rows = blocks[0].shape[0]
    total = nodes * rows
    for k in range(nodes):
        x_ref[k * rows : (k + 1) * rows, :] = blocks[k][...]
    x = x_ref[...]
    gram = dot_t(x, x)
    on_diagonal = lax.broadcasted_iota(jnp.int32, (total, total), 0) == lax.broadcasted_iota(
        jnp.int32, (total, total), 1
    )
    square = jnp.sum(jnp.where(on_diagonal, gram, 0.0))
    scale = 1.0 / (jnp.sqrt(jnp.full((1, 1), square, jnp.float32)) + 1e-07)
    gram = gram * scale * scale
    parts = row_parts(total)
    now = [gram[r] for r in parts]
    ortho = x
    for step in range(ITERS):
        low = [g.astype(jnp.bfloat16) for g in now]
        whole = jnp.concatenate(low, 0)
        poly = [coef_b * g + coef_c * dot(h, whole) for g, h in zip(now, low)]
        poly_low = [p.astype(jnp.bfloat16) for p in poly]
        poly_whole = jnp.concatenate(poly_low, 0)
        if step + 1 < ITERS:
            half = [coef_a * g + dot(p, whole) for g, p in zip(now, poly_low)]
            now = [coef_a * h + dot(h.astype(jnp.bfloat16), poly_whole) for h in half]
            ortho = (coef_a * ortho.astype(jnp.float32) + dot(poly_whole, ortho)).astype(jnp.bfloat16)
    rate = step_rate * math.sqrt(width)
    for k in range(nodes):
        r = slice(k * rows, (k + 1) * rows)
        change = dot(poly_whole[r], ortho) + coef_a * ortho[r].astype(jnp.float32)
        home = pl.ds(pl.multiple_of(at(come[k], me) * rows, rows), rows)
        out_ref[home, :] = (
            weight_ref[home, :].astype(jnp.float32) - (rate * scale) * change
        ).astype(jnp.bfloat16)


def project_kernel(come, width, *refs):
    nodes = len(come)
    me = lax.axis_index("fsdp")
    blocks, own_ref, partner_ref = refs[:nodes], refs[nodes], refs[nodes + 1]
    weight_ref, rows_ref, slot_ref = refs[nodes + 2], refs[nodes + 3], refs[nodes + 4]
    capacity = blocks[0].shape[0]
    weight = (
        0.5 * (own_ref[...].astype(jnp.float32) + partner_ref[...].astype(jnp.float32))
    ).astype(jnp.bfloat16)
    weight_ref[...] = weight
    for k in range(nodes):
        home = pl.ds(pl.multiple_of(at(come[k], me) * capacity, capacity), capacity)
        slot_ref[home, :] = blocks[k][...]
    rows_ref[...] = (dot_t(slot_ref[...], weight) * (1.0 / math.sqrt(width))).astype(jnp.bfloat16)


def per_device(momentum, weights, tokens, routes):
    nodes = lax.axis_size("fsdp")
    rows, width = momentum.shape[2], momentum.shape[3]
    total = weights.shape[2]
    tok_rows = tokens.shape[1]
    capacity = 2 * tok_rows // nodes
    here = tuple(range(nodes))
    far = [here, *steps(nodes, MH)]
    near = [here, *steps(nodes, TH)]

    source = pltpu.with_memory_space_constraint(momentum[0], pltpu.HBM)
    blocks = []
    for k, step in enumerate(far):
        shard = pl.pallas_call(
            functools.partial(slice_kernel, step),
            out_shape=jax.ShapeDtypeStruct((rows, width), jnp.bfloat16),
            in_specs=[pl.BlockSpec(memory_space=pltpu.HBM)],
            out_specs=VMEM,
            scratch_shapes=[pltpu.SemaphoreType.DMA],
            compiler_params=pltpu.CompilerParams(vmem_limit_bytes=8 << 20),
            name="slice",
        )(source)
        blocks.append(trade(shard, step) if k else shard)

    packed = list(
        pl.pallas_call(
            functools.partial(pack_kernel, near, capacity),
            out_shape=[jax.ShapeDtypeStruct((capacity, width), jnp.bfloat16)] * nodes,
            in_specs=[VMEM, VMEM],
            out_specs=[VMEM] * nodes,
            compiler_params=pltpu.CompilerParams(vmem_limit_bytes=16 << 20),
            cost_estimate=pl.CostEstimate(
                flops=2 * nodes * capacity * tok_rows * width,
                bytes_accessed=2 * (tok_rows + nodes * capacity) * width,
                transcendentals=0,
            ),
            name="pack",
        )(routes.reshape(1, tok_rows), tokens[0])
    )
    slots = [packed[0]]
    for k, step in enumerate(near[1:], 1):
        slots.append(trade(packed[k], step))

    updated = pl.pallas_call(
        functools.partial(update_kernel, [inverse(s) for s in far], width),
        out_shape=jax.ShapeDtypeStruct((total, width), jnp.bfloat16),
        in_specs=[VMEM] * (nodes + 1),
        out_specs=VMEM,
        scratch_shapes=[pltpu.VMEM((total, width), jnp.bfloat16)],
        compiler_params=pltpu.CompilerParams(vmem_limit_bytes=24 << 20),
        cost_estimate=pl.CostEstimate(
            flops=4 * total * total * width + 10 * total**3,
            bytes_accessed=6 * total * width,
            transcendentals=0,
        ),
        name="update",
    )(*blocks, weights[0, 0])
    partner = lax.ppermute(
        updated, "replica", [(i, i ^ 1 << GOSSIP_BIT) for i in range(lax.axis_size("replica"))]
    )
    averaged, expert_rows = pl.pallas_call(
        functools.partial(project_kernel, [inverse(s) for s in near], width),
        out_shape=(
            jax.ShapeDtypeStruct((total, width), jnp.bfloat16),
            jax.ShapeDtypeStruct((nodes * capacity, total), jnp.bfloat16),
        ),
        in_specs=[VMEM] * (nodes + 2),
        out_specs=(VMEM, VMEM),
        scratch_shapes=[pltpu.VMEM((nodes * capacity, width), jnp.bfloat16)],
        compiler_params=pltpu.CompilerParams(vmem_limit_bytes=24 << 20),
        cost_estimate=pl.CostEstimate(
            flops=2 * nodes * capacity * width * total,
            bytes_accessed=6 * total * width + 2 * nodes * capacity * (width + total),
            transcendentals=0,
        ),
        name="project",
    )(*slots, updated, partner)
    return (averaged[None, None], expert_rows[None, None])


def solution(mesh):
    in_specs = (
        P("replica", None, "fsdp", None),
        P("replica", "fsdp", None, None),
        P("replica", "fsdp", None),
        P("replica", "fsdp", None),
    )
    out_specs = (P("replica", "fsdp", None, None), P("replica", "fsdp", None, None))

    return jax.shard_map(per_device, mesh=mesh, in_specs=in_specs, out_specs=out_specs, check_vma=False)
```

```python
import functools
import math

import jax
import jax.numpy as jnp
from jax import lax
from jax.experimental import pallas as pl
from jax.experimental.pallas import tpu as pltpu
from jax.sharding import PartitionSpec as P


ITERS = 2
GOSSIP_BIT = 2


coef_a = 3.4445
coef_b = -4.775
coef_c = 2.0315
step_rate = 0.5
MH = ("c3", 1, "c1")
TH = (1, 2, 3)
STEPS = {
    1: (1, 0, 3, 2),
    2: (2, 3, 0, 1),
    3: (3, 2, 1, 0),
    "a1": (1, 2, 3, 0),
    "a3": (3, 0, 1, 2),
    "b1": (1, 3, 0, 2),
    "b3": (2, 0, 3, 1),
    "c1": (2, 3, 1, 0),
    "c3": (3, 2, 0, 1),
}

VMEM = pl.BlockSpec(memory_space=pltpu.VMEM)


def dot(a, b):
    return jnp.dot(a, b, preferred_element_type=jnp.float32)


def dot_t(a, b):
    return lax.dot_general(a, b, (((1,), (1,)), ((), ())), preferred_element_type=jnp.float32)


def steps(nodes, order):
    if nodes == 4:
        return [STEPS[k] for k in order]
    if nodes & (nodes - 1) == 0:
        return [tuple(i ^ k for i in range(nodes)) for k in (*range(2, nodes), 1)]
    return [tuple((i + k) % nodes for i in range(nodes)) for k in (*range(2, nodes), 1)]


def inverse(step):
    return tuple(step.index(i) for i in range(len(step)))


def at(step, me):
    hop = step[0]
    if all(to == i ^ hop for i, to in enumerate(step)):
        return me ^ hop
    found = step[0]
    for i, to in enumerate(step[1:], 1):
        found = jnp.where(me == i, to, found)
    return found


def trade(block, step):
    return lax.ppermute(block, "fsdp", list(enumerate(step)))


def slice_kernel(step, source_ref, out_ref, sem):
    cp = pltpu.make_async_copy(source_ref.at[at(step, lax.axis_index("fsdp"))], out_ref, sem)
    cp.start()
    cp.wait()


def pack_kernel(to, capacity, routes_ref, tokens_ref, *out_refs):
    tok_rows = routes_ref.shape[1]
    routes = routes_ref[...]
    me = lax.axis_index("fsdp")
    earlier = lax.broadcasted_iota(jnp.int32, (tok_rows, tok_rows), 0) < lax.broadcasted_iota(
        jnp.int32, (tok_rows, tok_rows), 1
    )
    earlier = jnp.where(earlier, 1.0, 0.0).astype(jnp.bfloat16)
    slot = lax.broadcasted_iota(jnp.int32, (capacity, tok_rows), 0)
    tokens = tokens_ref[...]
    for k, step in enumerate(to):
        here = routes == at(step, me)
        count = dot(jnp.where(here, 1.0, 0.0).astype(jnp.bfloat16), earlier)
        position = jnp.where(here, count.astype(jnp.int32), -1)
        placing = jnp.where(slot == position, 1.0, 0.0).astype(jnp.bfloat16)
        out_refs[k][...] = dot(placing, tokens).astype(jnp.bfloat16)


def row_parts(rows):
    part = 128 if rows % 128 == 0 else rows
    return [slice(i, i + part) for i in range(0, rows, part)]


def update_kernel(come, width, *refs):
    nodes = len(come)
    blocks, weight_ref, out_ref, x_ref = refs[:nodes], refs[nodes], refs[nodes + 1], refs[nodes + 2]
    me = lax.axis_index("fsdp")
    rows = blocks[0].shape[0]
    total = nodes * rows
    for k in range(nodes):
        x_ref[k * rows : (k + 1) * rows, :] = blocks[k][...]
    x = x_ref[...]
    gram = dot_t(x, x)
    on_diagonal = lax.broadcasted_iota(jnp.int32, (total, total), 0) == lax.broadcasted_iota(
        jnp.int32, (total, total), 1
    )
    square = jnp.sum(jnp.where(on_diagonal, gram, 0.0))
    scale = 1.0 / (jnp.sqrt(jnp.full((1, 1), square, jnp.float32)) + 1e-07)
    gram = gram * scale * scale
    parts = row_parts(total)
    now = [gram[r] for r in parts]
    ortho = x
    for step in range(ITERS):
        low = [g.astype(jnp.bfloat16) for g in now]
        whole = jnp.concatenate(low, 0)
        poly = [coef_b * g + coef_c * dot(h, whole) for g, h in zip(now, low)]
        poly_low = [p.astype(jnp.bfloat16) for p in poly]
        poly_whole = jnp.concatenate(poly_low, 0)
        if step + 1 < ITERS:
            half = [coef_a * g + dot(p, whole) for g, p in zip(now, poly_low)]
            now = [coef_a * h + dot(h.astype(jnp.bfloat16), poly_whole) for h in half]
            ortho = (coef_a * ortho.astype(jnp.float32) + dot(poly_whole, ortho)).astype(jnp.bfloat16)
    rate = step_rate * math.sqrt(width)
    for k in range(nodes):
        r = slice(k * rows, (k + 1) * rows)
        change = dot(poly_whole[r], ortho) + coef_a * ortho[r].astype(jnp.float32)
        home = pl.ds(pl.multiple_of(at(come[k], me) * rows, rows), rows)
        out_ref[home, :] = (
            weight_ref[home, :].astype(jnp.float32) - (rate * scale) * change
        ).astype(jnp.bfloat16)


def project_kernel(come, width, *refs):
    nodes = len(come)
    blocks, own_ref, partner_ref = refs[:nodes], refs[nodes], refs[nodes + 1]
    weight_out, rows_out, weight_ref, slot_ref, rows_ref, sems = refs[nodes + 2 :]
    me = lax.axis_index("fsdp")
    capacity = blocks[0].shape[0]
    weight = (
        0.5 * (own_ref[...].astype(jnp.float32) + partner_ref[...].astype(jnp.float32))
    ).astype(jnp.bfloat16)
    weight_ref[...] = weight
    copies = [pltpu.make_async_copy(weight_ref, weight_out, sems.at[nodes])]
    copies[0].start()
    for k in range(nodes):
        slot_ref[k * capacity : (k + 1) * capacity, :] = blocks[k][...]
    rows_ref[...] = (dot_t(slot_ref[...], weight) * (1.0 / math.sqrt(width))).astype(jnp.bfloat16)
    for k in range(nodes):
        home = pl.ds(pl.multiple_of(at(come[k], me) * capacity, capacity), capacity)
        copies.append(
            pltpu.make_async_copy(
                rows_ref.at[k * capacity : (k + 1) * capacity], rows_out.at[home], sems.at[k]
            )
        )
        copies[-1].start()
    for cp in copies:
        cp.wait()


def last_kernel(come, width, block_ref, weight_ref, _, rows_out, rows_ref, sem):
    me = lax.axis_index("fsdp")
    capacity = block_ref.shape[0]
    rows_ref[...] = (dot_t(block_ref[...], weight_ref[...]) * (1.0 / math.sqrt(width))).astype(
        jnp.bfloat16
    )
    home = pl.ds(pl.multiple_of(at(come, me) * capacity, capacity), capacity)
    cp = pltpu.make_async_copy(rows_ref, rows_out.at[home], sem)
    cp.start()
    cp.wait()


def per_device(momentum, weights, tokens, routes):
    nodes = lax.axis_size("fsdp")
    rows, width = momentum.shape[2], momentum.shape[3]
    total = weights.shape[2]
    tok_rows = tokens.shape[1]
    capacity = 2 * tok_rows // nodes
    here = tuple(range(nodes))
    far = [here, *steps(nodes, MH)]
    near = [here, *steps(nodes, TH)]

    source = pltpu.with_memory_space_constraint(momentum[0], pltpu.HBM)
    blocks = []
    for k, step in enumerate(far):
        shard = pl.pallas_call(
            functools.partial(slice_kernel, step),
            out_shape=jax.ShapeDtypeStruct((rows, width), jnp.bfloat16),
            in_specs=[pl.BlockSpec(memory_space=pltpu.HBM)],
            out_specs=VMEM,
            scratch_shapes=[pltpu.SemaphoreType.DMA],
            compiler_params=pltpu.CompilerParams(vmem_limit_bytes=8 << 20),
            name="slice",
        )(source)
        blocks.append(trade(shard, step) if k else shard)

    packed = list(
        pl.pallas_call(
            functools.partial(pack_kernel, near, capacity),
            out_shape=[jax.ShapeDtypeStruct((capacity, width), jnp.bfloat16)] * nodes,
            in_specs=[VMEM, VMEM],
            out_specs=[VMEM] * nodes,
            compiler_params=pltpu.CompilerParams(vmem_limit_bytes=16 << 20),
            cost_estimate=pl.CostEstimate(
                flops=2 * nodes * capacity * tok_rows * width,
                bytes_accessed=2 * (tok_rows + nodes * capacity) * width,
                transcendentals=0,
            ),
            name="pack",
        )(routes.reshape(1, tok_rows), tokens[0])
    )
    slots = [packed[0]]
    for k, step in enumerate(near[1:], 1):
        slots.append(trade(packed[k], step))

    updated = pl.pallas_call(
        functools.partial(update_kernel, [inverse(s) for s in far], width),
        out_shape=jax.ShapeDtypeStruct((total, width), jnp.bfloat16),
        in_specs=[VMEM] * (nodes + 1),
        out_specs=VMEM,
        scratch_shapes=[pltpu.VMEM((total, width), jnp.bfloat16)],
        compiler_params=pltpu.CompilerParams(vmem_limit_bytes=24 << 20),
        cost_estimate=pl.CostEstimate(
            flops=4 * total * total * width + 10 * total**3,
            bytes_accessed=6 * total * width,
            transcendentals=0,
        ),
        name="update",
    )(*blocks, weights[0, 0])
    partner = lax.ppermute(
        updated, "replica", [(i, i ^ 1 << GOSSIP_BIT) for i in range(lax.axis_size("replica"))]
    )
    come = [inverse(step) for step in near]
    early = nodes - 1
    rows_shape = jax.ShapeDtypeStruct((nodes * capacity, total), jnp.bfloat16)
    hbm = pl.BlockSpec(memory_space=pltpu.HBM)
    averaged, expert_rows, kept = pl.pallas_call(
        functools.partial(project_kernel, come[:early], width),
        out_shape=(
            jax.ShapeDtypeStruct((total, width), jnp.bfloat16),
            rows_shape,
            jax.ShapeDtypeStruct((total, width), jnp.bfloat16),
        ),
        in_specs=[VMEM] * (early + 2),
        out_specs=(hbm, hbm, VMEM),
        scratch_shapes=[
            pltpu.VMEM((early * capacity, width), jnp.bfloat16),
            pltpu.VMEM((early * capacity, total), jnp.bfloat16),
            pltpu.SemaphoreType.DMA((nodes,)),
        ],
        compiler_params=pltpu.CompilerParams(vmem_limit_bytes=24 << 20),
        cost_estimate=pl.CostEstimate(
            flops=2 * early * capacity * width * total,
            bytes_accessed=6 * total * width + 2 * early * capacity * (width + total),
            transcendentals=0,
        ),
        name="project",
    )(*slots[:early], updated, partner)
    expert_rows = pl.pallas_call(
        functools.partial(last_kernel, come[early], width),
        out_shape=rows_shape,
        in_specs=[VMEM, VMEM, hbm],
        out_specs=hbm,
        scratch_shapes=[
            pltpu.VMEM((capacity, total), jnp.bfloat16),
            pltpu.SemaphoreType.DMA,
        ],
        input_output_aliases={2: 0},
        compiler_params=pltpu.CompilerParams(vmem_limit_bytes=24 << 20),
        cost_estimate=pl.CostEstimate(
            flops=2 * capacity * width * total,
            bytes_accessed=2 * capacity * (width + total),
            transcendentals=0,
        ),
        name="last",
    )(slots[early], kept, expert_rows)
    return (averaged[None, None], expert_rows[None, None])


def solution(mesh):
    in_specs = (
        P("replica", None, "fsdp", None),
        P("replica", "fsdp", None, None),
        P("replica", "fsdp", None),
        P("replica", "fsdp", None),
    )
    out_specs = (P("replica", "fsdp", None, None), P("replica", "fsdp", None, None))

    return jax.shard_map(per_device, mesh=mesh, in_specs=in_specs, out_specs=out_specs, check_vma=False)
```

```python
import functools
import math

import jax
import jax.numpy as jnp
from jax import lax
from jax.experimental import pallas as pl
from jax.experimental.pallas import tpu as pltpu
from jax.sharding import PartitionSpec as P


ITERS = 2
GOSSIP_BIT = 2


coef_a = 3.4445
coef_b = -4.775
coef_c = 2.0315
step_rate = 0.5
MH = ("c3", 1, "c1")
TH = (1, "c3", "c1")
STEPS = {
    1: (1, 0, 3, 2),
    2: (2, 3, 0, 1),
    3: (3, 2, 1, 0),
    "a1": (1, 2, 3, 0),
    "a3": (3, 0, 1, 2),
    "b1": (1, 3, 0, 2),
    "b3": (2, 0, 3, 1),
    "c1": (2, 3, 1, 0),
    "c3": (3, 2, 0, 1),
}

VMEM = pl.BlockSpec(memory_space=pltpu.VMEM)


def dot(a, b):
    return jnp.dot(a, b, preferred_element_type=jnp.float32)


def dot_t(a, b):
    return lax.dot_general(a, b, (((1,), (1,)), ((), ())), preferred_element_type=jnp.float32)


def steps(nodes, order):
    if nodes == 4:
        return [STEPS[k] for k in order]
    if nodes & (nodes - 1) == 0:
        return [tuple(i ^ k for i in range(nodes)) for k in (*range(2, nodes), 1)]
    return [tuple((i + k) % nodes for i in range(nodes)) for k in (*range(2, nodes), 1)]


def inverse(step):
    return tuple(step.index(i) for i in range(len(step)))


def at(step, me):
    hop = step[0]
    if all(to == i ^ hop for i, to in enumerate(step)):
        return me ^ hop
    found = step[0]
    for i, to in enumerate(step[1:], 1):
        found = jnp.where(me == i, to, found)
    return found


def trade(block, step):
    return lax.ppermute(block, "fsdp", list(enumerate(step)))


def slice_kernel(step, source_ref, out_ref, sem):
    cp = pltpu.make_async_copy(source_ref.at[at(step, lax.axis_index("fsdp"))], out_ref, sem)
    cp.start()
    cp.wait()


def pack_kernel(to, capacity, routes_ref, tokens_ref, *out_refs):
    tok_rows = routes_ref.shape[1]
    routes = routes_ref[...]
    me = lax.axis_index("fsdp")
    earlier = lax.broadcasted_iota(jnp.int32, (tok_rows, tok_rows), 0) < lax.broadcasted_iota(
        jnp.int32, (tok_rows, tok_rows), 1
    )
    earlier = jnp.where(earlier, 1.0, 0.0).astype(jnp.bfloat16)
    slot = lax.broadcasted_iota(jnp.int32, (capacity, tok_rows), 0)
    tokens = tokens_ref[...]
    for k, step in enumerate(to):
        here = routes == at(step, me)
        count = dot(jnp.where(here, 1.0, 0.0).astype(jnp.bfloat16), earlier)
        position = jnp.where(here, count.astype(jnp.int32), -1)
        placing = jnp.where(slot == position, 1.0, 0.0).astype(jnp.bfloat16)
        out_refs[k][...] = dot(placing, tokens).astype(jnp.bfloat16)


def row_parts(rows):
    part = 128 if rows % 128 == 0 else rows
    return [slice(i, i + part) for i in range(0, rows, part)]


def update_kernel(come, width, *refs):
    nodes = len(come)
    blocks, weight_ref, out_ref, x_ref = refs[:nodes], refs[nodes], refs[nodes + 1], refs[nodes + 2]
    me = lax.axis_index("fsdp")
    rows = blocks[0].shape[0]
    total = nodes * rows
    for k in range(nodes):
        x_ref[k * rows : (k + 1) * rows, :] = blocks[k][...]
    x = x_ref[...]
    gram = dot_t(x, x)
    on_diagonal = lax.broadcasted_iota(jnp.int32, (total, total), 0) == lax.broadcasted_iota(
        jnp.int32, (total, total), 1
    )
    square = jnp.sum(jnp.where(on_diagonal, gram, 0.0))
    scale = 1.0 / (jnp.sqrt(jnp.full((1, 1), square, jnp.float32)) + 1e-07)
    gram = gram * scale * scale
    parts = row_parts(total)
    now = [gram[r] for r in parts]
    ortho = x
    for step in range(ITERS):
        low = [g.astype(jnp.bfloat16) for g in now]
        whole = jnp.concatenate(low, 0)
        poly = [coef_b * g + coef_c * dot(h, whole) for g, h in zip(now, low)]
        poly_low = [p.astype(jnp.bfloat16) for p in poly]
        poly_whole = jnp.concatenate(poly_low, 0)
        if step + 1 < ITERS:
            half = [coef_a * g + dot(p, whole) for g, p in zip(now, poly_low)]
            now = [coef_a * h + dot(h.astype(jnp.bfloat16), poly_whole) for h in half]
            ortho = (coef_a * ortho.astype(jnp.float32) + dot(poly_whole, ortho)).astype(jnp.bfloat16)
    rate = step_rate * math.sqrt(width)
    for k in range(nodes):
        r = slice(k * rows, (k + 1) * rows)
        change = dot(poly_whole[r], ortho) + coef_a * ortho[r].astype(jnp.float32)
        home = pl.ds(pl.multiple_of(at(come[k], me) * rows, rows), rows)
        out_ref[home, :] = (
            weight_ref[home, :].astype(jnp.float32) - (rate * scale) * change
        ).astype(jnp.bfloat16)


def project_kernel(come, width, *refs):
    nodes = len(come)
    blocks, own_ref, partner_ref = refs[:nodes], refs[nodes], refs[nodes + 1]
    weight_out, rows_out, turned_ref, weight_ref, slot_ref, rows_ref, sems = refs[nodes + 2 :]
    me = lax.axis_index("fsdp")
    capacity = blocks[0].shape[0]
    weight = (
        0.5 * (own_ref[...].astype(jnp.float32) + partner_ref[...].astype(jnp.float32))
    ).astype(jnp.bfloat16)
    weight_ref[...] = weight
    copies = [pltpu.make_async_copy(weight_ref, weight_out, sems.at[nodes])]
    copies[0].start()
    for k in range(nodes):
        slot_ref[k * capacity : (k + 1) * capacity, :] = blocks[k][...]
    rows_ref[...] = (dot_t(slot_ref[...], weight) * (1.0 / math.sqrt(width))).astype(jnp.bfloat16)
    for k in range(nodes):
        home = pl.ds(pl.multiple_of(at(come[k], me) * capacity, capacity), capacity)
        copies.append(
            pltpu.make_async_copy(
                rows_ref.at[k * capacity : (k + 1) * capacity], rows_out.at[home], sems.at[k]
            )
        )
        copies[-1].start()
    turned_ref[...] = weight.T
    for cp in copies:
        cp.wait()


def last_kernel(come, width, block_ref, turned_ref, _, rows_out, rows_ref, sem):
    me = lax.axis_index("fsdp")
    capacity = block_ref.shape[0]
    rows_ref[...] = (dot(block_ref[...], turned_ref[...]) * (1.0 / math.sqrt(width))).astype(
        jnp.bfloat16
    )
    home = pl.ds(pl.multiple_of(at(come, me) * capacity, capacity), capacity)
    cp = pltpu.make_async_copy(rows_ref, rows_out.at[home], sem)
    cp.start()
    cp.wait()


def per_device(momentum, weights, tokens, routes):
    nodes = lax.axis_size("fsdp")
    rows, width = momentum.shape[2], momentum.shape[3]
    total = weights.shape[2]
    tok_rows = tokens.shape[1]
    capacity = 2 * tok_rows // nodes
    here = tuple(range(nodes))
    far = [here, *steps(nodes, MH)]
    near = [here, *steps(nodes, TH)]

    source = pltpu.with_memory_space_constraint(momentum[0], pltpu.HBM)
    blocks = []
    for k, step in enumerate(far):
        shard = pl.pallas_call(
            functools.partial(slice_kernel, step),
            out_shape=jax.ShapeDtypeStruct((rows, width), jnp.bfloat16),
            in_specs=[pl.BlockSpec(memory_space=pltpu.HBM)],
            out_specs=VMEM,
            scratch_shapes=[pltpu.SemaphoreType.DMA],
            compiler_params=pltpu.CompilerParams(vmem_limit_bytes=8 << 20),
            name="slice",
        )(source)
        blocks.append(trade(shard, step) if k else shard)

    packed = list(
        pl.pallas_call(
            functools.partial(pack_kernel, near, capacity),
            out_shape=[jax.ShapeDtypeStruct((capacity, width), jnp.bfloat16)] * nodes,
            in_specs=[VMEM, VMEM],
            out_specs=[VMEM] * nodes,
            compiler_params=pltpu.CompilerParams(vmem_limit_bytes=16 << 20),
            cost_estimate=pl.CostEstimate(
                flops=2 * nodes * capacity * tok_rows * width,
                bytes_accessed=2 * (tok_rows + nodes * capacity) * width,
                transcendentals=0,
            ),
            name="pack",
        )(routes.reshape(1, tok_rows), tokens[0])
    )
    slots = [packed[0]]
    for k, step in enumerate(near[1:], 1):
        slots.append(trade(packed[k], step))

    updated = pl.pallas_call(
        functools.partial(update_kernel, [inverse(s) for s in far], width),
        out_shape=jax.ShapeDtypeStruct((total, width), jnp.bfloat16),
        in_specs=[VMEM] * (nodes + 1),
        out_specs=VMEM,
        scratch_shapes=[pltpu.VMEM((total, width), jnp.bfloat16)],
        compiler_params=pltpu.CompilerParams(vmem_limit_bytes=24 << 20),
        cost_estimate=pl.CostEstimate(
            flops=4 * total * total * width + 10 * total**3,
            bytes_accessed=6 * total * width,
            transcendentals=0,
        ),
        name="update",
    )(*blocks, weights[0, 0])
    partner = lax.ppermute(
        updated, "replica", [(i, i ^ 1 << GOSSIP_BIT) for i in range(lax.axis_size("replica"))]
    )
    come = [inverse(step) for step in near]
    early = nodes - 1
    rows_shape = jax.ShapeDtypeStruct((nodes * capacity, total), jnp.bfloat16)
    hbm = pl.BlockSpec(memory_space=pltpu.HBM)
    averaged, expert_rows, kept = pl.pallas_call(
        functools.partial(project_kernel, come[:early], width),
        out_shape=(
            jax.ShapeDtypeStruct((total, width), jnp.bfloat16),
            rows_shape,
            jax.ShapeDtypeStruct((width, total), jnp.bfloat16),
        ),
        in_specs=[VMEM] * (early + 2),
        out_specs=(hbm, hbm, VMEM),
        scratch_shapes=[
            pltpu.VMEM((total, width), jnp.bfloat16),
            pltpu.VMEM((early * capacity, width), jnp.bfloat16),
            pltpu.VMEM((early * capacity, total), jnp.bfloat16),
            pltpu.SemaphoreType.DMA((nodes,)),
        ],
        compiler_params=pltpu.CompilerParams(vmem_limit_bytes=24 << 20),
        cost_estimate=pl.CostEstimate(
            flops=2 * early * capacity * width * total,
            bytes_accessed=6 * total * width + 2 * early * capacity * (width + total),
            transcendentals=0,
        ),
        name="project",
    )(*slots[:early], updated, partner)
    expert_rows = pl.pallas_call(
        functools.partial(last_kernel, come[early], width),
        out_shape=rows_shape,
        in_specs=[VMEM, VMEM, hbm],
        out_specs=hbm,
        scratch_shapes=[
            pltpu.VMEM((capacity, total), jnp.bfloat16),
            pltpu.SemaphoreType.DMA,
        ],
        input_output_aliases={2: 0},
        compiler_params=pltpu.CompilerParams(vmem_limit_bytes=24 << 20),
        cost_estimate=pl.CostEstimate(
            flops=2 * capacity * width * total,
            bytes_accessed=2 * capacity * (width + total),
            transcendentals=0,
        ),
        name="last",
    )(slots[early], kept, expert_rows)
    return (averaged[None, None], expert_rows[None, None])


def solution(mesh):
    in_specs = (
        P("replica", None, "fsdp", None),
        P("replica", "fsdp", None, None),
        P("replica", "fsdp", None),
        P("replica", "fsdp", None),
    )
    out_specs = (P("replica", "fsdp", None, None), P("replica", "fsdp", None, None))

    return jax.shard_map(per_device, mesh=mesh, in_specs=in_specs, out_specs=out_specs, check_vma=False)
```

```python
import functools
import math

import jax
import jax.numpy as jnp
from jax import lax
from jax.experimental import pallas as pl
from jax.experimental.pallas import tpu as pltpu
from jax.sharding import PartitionSpec as P


ITERS = 2
GOSSIP_BIT = 2


coef_a = 3.4445
coef_b = -4.775
coef_c = 2.0315
step_rate = 0.5
MH = (("b3", "b1", 3), ("c3", 1, "c1"))
TH = ((1, "c3", "c1"), (1, "c3", "c1"))
STEPS = {
    1: (1, 0, 3, 2),
    2: (2, 3, 0, 1),
    3: (3, 2, 1, 0),
    "a1": (1, 2, 3, 0),
    "a3": (3, 0, 1, 2),
    "b1": (1, 3, 0, 2),
    "b3": (2, 0, 3, 1),
    "c1": (2, 3, 1, 0),
    "c3": (3, 2, 0, 1),
}

VMEM = pl.BlockSpec(memory_space=pltpu.VMEM)


def dot(a, b):
    return jnp.dot(a, b, preferred_element_type=jnp.float32)


def dot_t(a, b):
    return lax.dot_general(a, b, (((1,), (1,)), ((), ())), preferred_element_type=jnp.float32)


def steps(nodes, order):
    if nodes == 4:
        return [STEPS[k] for k in order]
    if nodes & (nodes - 1) == 0:
        return [tuple(i ^ k for i in range(nodes)) for k in (*range(2, nodes), 1)]
    return [tuple((i + k) % nodes for i in range(nodes)) for k in (*range(2, nodes), 1)]


def inverse(pair):
    return tuple(tuple(step.index(i) for i in range(len(step))) for step in pair)


def entry(step, me):
    hop = step[0]
    if all(to == i ^ hop for i, to in enumerate(step)):
        return me ^ hop
    found = step[0]
    for i, to in enumerate(step[1:], 1):
        found = jnp.where(me == i, to, found)
    return found


def at(pair, me):
    even, odd = pair
    if even == odd:
        return entry(even, me)
    return jnp.where(lax.axis_index("replica") % 2 == 0, entry(even, me), entry(odd, me))


def trade(block, pair):
    nodes = len(pair[0])
    pairs = [
        (r * nodes + i, r * nodes + to)
        for r in range(lax.axis_size("replica"))
        for i, to in enumerate(pair[r % 2])
    ]
    return lax.ppermute(block, ("replica", "fsdp"), pairs)


def slice_kernel(step, source_ref, out_ref, sem):
    cp = pltpu.make_async_copy(source_ref.at[at(step, lax.axis_index("fsdp"))], out_ref, sem)
    cp.start()
    cp.wait()


def pack_kernel(to, capacity, routes_ref, tokens_ref, *out_refs):
    tok_rows = routes_ref.shape[1]
    routes = routes_ref[...]
    me = lax.axis_index("fsdp")
    earlier = lax.broadcasted_iota(jnp.int32, (tok_rows, tok_rows), 0) < lax.broadcasted_iota(
        jnp.int32, (tok_rows, tok_rows), 1
    )
    earlier = jnp.where(earlier, 1.0, 0.0).astype(jnp.bfloat16)
    slot = lax.broadcasted_iota(jnp.int32, (capacity, tok_rows), 0)
    tokens = tokens_ref[...]
    for k, step in enumerate(to):
        here = routes == at(step, me)
        count = dot(jnp.where(here, 1.0, 0.0).astype(jnp.bfloat16), earlier)
        position = jnp.where(here, count.astype(jnp.int32), -1)
        placing = jnp.where(slot == position, 1.0, 0.0).astype(jnp.bfloat16)
        out_refs[k][...] = dot(placing, tokens).astype(jnp.bfloat16)


def row_parts(rows):
    part = 128 if rows % 128 == 0 else rows
    return [slice(i, i + part) for i in range(0, rows, part)]


def update_kernel(come, width, *refs):
    nodes = len(come)
    blocks, weight_ref, out_ref, x_ref = refs[:nodes], refs[nodes], refs[nodes + 1], refs[nodes + 2]
    me = lax.axis_index("fsdp")
    rows = blocks[0].shape[0]
    total = nodes * rows
    for k in range(nodes):
        x_ref[k * rows : (k + 1) * rows, :] = blocks[k][...]
    x = x_ref[...]
    gram = dot_t(x, x)
    on_diagonal = lax.broadcasted_iota(jnp.int32, (total, total), 0) == lax.broadcasted_iota(
        jnp.int32, (total, total), 1
    )
    square = jnp.sum(jnp.where(on_diagonal, gram, 0.0))
    scale = 1.0 / (jnp.sqrt(jnp.full((1, 1), square, jnp.float32)) + 1e-07)
    gram = gram * scale * scale
    parts = row_parts(total)
    now = [gram[r] for r in parts]
    ortho = x
    for step in range(ITERS):
        low = [g.astype(jnp.bfloat16) for g in now]
        whole = jnp.concatenate(low, 0)
        poly = [coef_b * g + coef_c * dot(h, whole) for g, h in zip(now, low)]
        poly_low = [p.astype(jnp.bfloat16) for p in poly]
        poly_whole = jnp.concatenate(poly_low, 0)
        if step + 1 < ITERS:
            half = [coef_a * g + dot(p, whole) for g, p in zip(now, poly_low)]
            now = [coef_a * h + dot(h.astype(jnp.bfloat16), poly_whole) for h in half]
            ortho = (coef_a * ortho.astype(jnp.float32) + dot(poly_whole, ortho)).astype(jnp.bfloat16)
    rate = step_rate * math.sqrt(width)
    for k in range(nodes):
        r = slice(k * rows, (k + 1) * rows)
        change = dot(poly_whole[r], ortho) + coef_a * ortho[r].astype(jnp.float32)
        home = pl.ds(pl.multiple_of(at(come[k], me) * rows, rows), rows)
        out_ref[home, :] = (
            weight_ref[home, :].astype(jnp.float32) - (rate * scale) * change
        ).astype(jnp.bfloat16)


def project_kernel(come, width, *refs):
    nodes = len(come)
    blocks, own_ref, partner_ref = refs[:nodes], refs[nodes], refs[nodes + 1]
    weight_out, rows_out, turned_ref, weight_ref, slot_ref, rows_ref, sems = refs[nodes + 2 :]
    me = lax.axis_index("fsdp")
    capacity = blocks[0].shape[0]
    weight = (
        0.5 * (own_ref[...].astype(jnp.float32) + partner_ref[...].astype(jnp.float32))
    ).astype(jnp.bfloat16)
    weight_ref[...] = weight
    copies = [pltpu.make_async_copy(weight_ref, weight_out, sems.at[nodes])]
    copies[0].start()
    for k in range(nodes):
        slot_ref[k * capacity : (k + 1) * capacity, :] = blocks[k][...]
    rows_ref[...] = (dot_t(slot_ref[...], weight) * (1.0 / math.sqrt(width))).astype(jnp.bfloat16)
    for k in range(nodes):
        home = pl.ds(pl.multiple_of(at(come[k], me) * capacity, capacity), capacity)
        copies.append(
            pltpu.make_async_copy(
                rows_ref.at[k * capacity : (k + 1) * capacity], rows_out.at[home], sems.at[k]
            )
        )
        copies[-1].start()
    turned_ref[...] = weight.T
    for cp in copies:
        cp.wait()


def last_kernel(come, width, block_ref, turned_ref, _, rows_out, rows_ref, sem):
    me = lax.axis_index("fsdp")
    capacity = block_ref.shape[0]
    rows_ref[...] = (dot(block_ref[...], turned_ref[...]) * (1.0 / math.sqrt(width))).astype(
        jnp.bfloat16
    )
    home = pl.ds(pl.multiple_of(at(come, me) * capacity, capacity), capacity)
    cp = pltpu.make_async_copy(rows_ref, rows_out.at[home], sem)
    cp.start()
    cp.wait()


def per_device(momentum, weights, tokens, routes):
    nodes = lax.axis_size("fsdp")
    rows, width = momentum.shape[2], momentum.shape[3]
    total = weights.shape[2]
    tok_rows = tokens.shape[1]
    capacity = 2 * tok_rows // nodes
    here = (tuple(range(nodes)),) * 2
    far = [here, *zip(*(steps(nodes, order) for order in MH))]
    near = [here, *zip(*(steps(nodes, order) for order in TH))]

    source = pltpu.with_memory_space_constraint(momentum[0], pltpu.HBM)
    blocks = []
    for k, step in enumerate(far):
        shard = pl.pallas_call(
            functools.partial(slice_kernel, step),
            out_shape=jax.ShapeDtypeStruct((rows, width), jnp.bfloat16),
            in_specs=[pl.BlockSpec(memory_space=pltpu.HBM)],
            out_specs=VMEM,
            scratch_shapes=[pltpu.SemaphoreType.DMA],
            compiler_params=pltpu.CompilerParams(vmem_limit_bytes=8 << 20),
            name="slice",
        )(source)
        blocks.append(trade(shard, step) if k else shard)

    packed = list(
        pl.pallas_call(
            functools.partial(pack_kernel, near, capacity),
            out_shape=[jax.ShapeDtypeStruct((capacity, width), jnp.bfloat16)] * nodes,
            in_specs=[VMEM, VMEM],
            out_specs=[VMEM] * nodes,
            compiler_params=pltpu.CompilerParams(vmem_limit_bytes=16 << 20),
            cost_estimate=pl.CostEstimate(
                flops=2 * nodes * capacity * tok_rows * width,
                bytes_accessed=2 * (tok_rows + nodes * capacity) * width,
                transcendentals=0,
            ),
            name="pack",
        )(routes.reshape(1, tok_rows), tokens[0])
    )
    slots = [packed[0]]
    for k, step in enumerate(near[1:], 1):
        slots.append(trade(packed[k], step))

    updated = pl.pallas_call(
        functools.partial(update_kernel, [inverse(s) for s in far], width),
        out_shape=jax.ShapeDtypeStruct((total, width), jnp.bfloat16),
        in_specs=[VMEM] * (nodes + 1),
        out_specs=VMEM,
        scratch_shapes=[pltpu.VMEM((total, width), jnp.bfloat16)],
        compiler_params=pltpu.CompilerParams(vmem_limit_bytes=24 << 20),
        cost_estimate=pl.CostEstimate(
            flops=4 * total * total * width + 10 * total**3,
            bytes_accessed=6 * total * width,
            transcendentals=0,
        ),
        name="update",
    )(*blocks, weights[0, 0])
    partner = lax.ppermute(
        updated, "replica", [(i, i ^ 1 << GOSSIP_BIT) for i in range(lax.axis_size("replica"))]
    )
    come = [inverse(step) for step in near]
    early = nodes - 1
    rows_shape = jax.ShapeDtypeStruct((nodes * capacity, total), jnp.bfloat16)
    hbm = pl.BlockSpec(memory_space=pltpu.HBM)
    averaged, expert_rows, kept = pl.pallas_call(
        functools.partial(project_kernel, come[:early], width),
        out_shape=(
            jax.ShapeDtypeStruct((total, width), jnp.bfloat16),
            rows_shape,
            jax.ShapeDtypeStruct((width, total), jnp.bfloat16),
        ),
        in_specs=[VMEM] * (early + 2),
        out_specs=(hbm, hbm, VMEM),
        scratch_shapes=[
            pltpu.VMEM((total, width), jnp.bfloat16),
            pltpu.VMEM((early * capacity, width), jnp.bfloat16),
            pltpu.VMEM((early * capacity, total), jnp.bfloat16),
            pltpu.SemaphoreType.DMA((nodes,)),
        ],
        compiler_params=pltpu.CompilerParams(vmem_limit_bytes=24 << 20),
        cost_estimate=pl.CostEstimate(
            flops=2 * early * capacity * width * total,
            bytes_accessed=6 * total * width + 2 * early * capacity * (width + total),
            transcendentals=0,
        ),
        name="project",
    )(*slots[:early], updated, partner)
    expert_rows = pl.pallas_call(
        functools.partial(last_kernel, come[early], width),
        out_shape=rows_shape,
        in_specs=[VMEM, VMEM, hbm],
        out_specs=hbm,
        scratch_shapes=[
            pltpu.VMEM((capacity, total), jnp.bfloat16),
            pltpu.SemaphoreType.DMA,
        ],
        input_output_aliases={2: 0},
        compiler_params=pltpu.CompilerParams(vmem_limit_bytes=24 << 20),
        cost_estimate=pl.CostEstimate(
            flops=2 * capacity * width * total,
            bytes_accessed=2 * capacity * (width + total),
            transcendentals=0,
        ),
        name="last",
    )(slots[early], kept, expert_rows)
    return (averaged[None, None], expert_rows[None, None])


def solution(mesh):
    in_specs = (
        P("replica", None, "fsdp", None),
        P("replica", "fsdp", None, None),
        P("replica", "fsdp", None),
        P("replica", "fsdp", None),
    )
    out_specs = (P("replica", "fsdp", None, None), P("replica", "fsdp", None, None))

    return jax.shard_map(per_device, mesh=mesh, in_specs=in_specs, out_specs=out_specs, check_vma=False)
```

```python
import functools
import math

import jax
import jax.numpy as jnp
from jax import lax
from jax.experimental import pallas as pl
from jax.experimental.pallas import tpu as pltpu
from jax.sharding import PartitionSpec as P


ITERS = 2
GOSSIP_BIT = 2


coef_a = 3.4445
coef_b = -4.775
coef_c = 2.0315
step_rate = 0.5
MH = (("b3", "b1", 3), ("c3", 1, "c1"))
TH = ((1, "c3", "c1"), (1, "c3", "c1"))
STEPS = {
    1: (1, 0, 3, 2),
    2: (2, 3, 0, 1),
    3: (3, 2, 1, 0),
    "a1": (1, 2, 3, 0),
    "a3": (3, 0, 1, 2),
    "b1": (1, 3, 0, 2),
    "b3": (2, 0, 3, 1),
    "c1": (2, 3, 1, 0),
    "c3": (3, 2, 0, 1),
}

VMEM = pl.BlockSpec(memory_space=pltpu.VMEM)


def dot(a, b):
    return jnp.dot(a, b, preferred_element_type=jnp.float32)


def dot_t(a, b):
    return lax.dot_general(a, b, (((1,), (1,)), ((), ())), preferred_element_type=jnp.float32)


def steps(nodes, order):
    if nodes == 4:
        return [STEPS[k] for k in order]
    if nodes & (nodes - 1) == 0:
        return [tuple(i ^ k for i in range(nodes)) for k in (*range(2, nodes), 1)]
    return [tuple((i + k) % nodes for i in range(nodes)) for k in (*range(2, nodes), 1)]


def inverse(pair):
    return tuple(tuple(step.index(i) for i in range(len(step))) for step in pair)


def entry(step, me):
    hop = step[0]
    if all(to == i ^ hop for i, to in enumerate(step)):
        return me ^ hop
    found = step[0]
    for i, to in enumerate(step[1:], 1):
        found = jnp.where(me == i, to, found)
    return found


def at(pair, me):
    even, odd = pair
    if even == odd:
        return entry(even, me)
    return jnp.where(lax.axis_index("replica") % 2 == 0, entry(even, me), entry(odd, me))


def trade(block, pair):
    nodes = len(pair[0])
    pairs = [
        (r * nodes + i, r * nodes + to)
        for r in range(lax.axis_size("replica"))
        for i, to in enumerate(pair[r % 2])
    ]
    return lax.ppermute(block, ("replica", "fsdp"), pairs)


def slice_kernel(step, source_ref, out_ref, sem):
    cp = pltpu.make_async_copy(source_ref.at[at(step, lax.axis_index("fsdp"))], out_ref, sem)
    cp.start()
    cp.wait()


def pack_kernel(to, capacity, routes_ref, tokens_ref, *out_refs):
    tok_rows = routes_ref.shape[1]
    routes = routes_ref[...]
    me = lax.axis_index("fsdp")
    earlier = lax.broadcasted_iota(jnp.int32, (tok_rows, tok_rows), 0) < lax.broadcasted_iota(
        jnp.int32, (tok_rows, tok_rows), 1
    )
    earlier = jnp.where(earlier, 1.0, 0.0).astype(jnp.bfloat16)
    slot = lax.broadcasted_iota(jnp.int32, (capacity, tok_rows), 0)
    tokens = tokens_ref[...]
    for k, step in enumerate(to):
        here = routes == at(step, me)
        count = dot(jnp.where(here, 1.0, 0.0).astype(jnp.bfloat16), earlier)
        position = jnp.where(here, count.astype(jnp.int32), -1)
        placing = jnp.where(slot == position, 1.0, 0.0).astype(jnp.bfloat16)
        block = dot(placing, tokens).astype(jnp.bfloat16)
        if k + 1 < len(to):
            out_refs[k][...] = block
        else:
            cut = out_refs[k].shape[1]
            out_refs[k][...] = block[:, :cut]
            out_refs[k + 1][...] = block[:, cut:]


def row_parts(rows):
    part = 128 if rows % 128 == 0 else rows
    return [slice(i, i + part) for i in range(0, rows, part)]


def update_kernel(come, width, *refs):
    nodes = len(come)
    blocks, weight_ref, out_ref, x_ref = refs[:nodes], refs[nodes], refs[nodes + 1], refs[nodes + 2]
    me = lax.axis_index("fsdp")
    rows = blocks[0].shape[0]
    total = nodes * rows
    for k in range(nodes):
        x_ref[k * rows : (k + 1) * rows, :] = blocks[k][...]
    x = x_ref[...]
    gram = dot_t(x, x)
    on_diagonal = lax.broadcasted_iota(jnp.int32, (total, total), 0) == lax.broadcasted_iota(
        jnp.int32, (total, total), 1
    )
    square = jnp.sum(jnp.where(on_diagonal, gram, 0.0))
    scale = 1.0 / (jnp.sqrt(jnp.full((1, 1), square, jnp.float32)) + 1e-07)
    gram = gram * scale * scale
    parts = row_parts(total)
    now = [gram[r] for r in parts]
    ortho = x
    for step in range(ITERS):
        low = [g.astype(jnp.bfloat16) for g in now]
        whole = jnp.concatenate(low, 0)
        poly = [coef_b * g + coef_c * dot(h, whole) for g, h in zip(now, low)]
        poly_low = [p.astype(jnp.bfloat16) for p in poly]
        poly_whole = jnp.concatenate(poly_low, 0)
        if step + 1 < ITERS:
            half = [coef_a * g + dot(p, whole) for g, p in zip(now, poly_low)]
            now = [coef_a * h + dot(h.astype(jnp.bfloat16), poly_whole) for h in half]
            ortho = (coef_a * ortho.astype(jnp.float32) + dot(poly_whole, ortho)).astype(jnp.bfloat16)
    rate = step_rate * math.sqrt(width)
    for k in range(nodes):
        r = slice(k * rows, (k + 1) * rows)
        change = dot(poly_whole[r], ortho) + coef_a * ortho[r].astype(jnp.float32)
        home = pl.ds(pl.multiple_of(at(come[k], me) * rows, rows), rows)
        out_ref[home, :] = (
            weight_ref[home, :].astype(jnp.float32) - (rate * scale) * change
        ).astype(jnp.bfloat16)


def project_kernel(come, width, *refs):
    nodes = len(come)
    blocks, own_ref, partner_ref = refs[:nodes], *refs[nodes : nodes + 2]
    weight_out, rows_out, turned_ref, weight_ref, slot_ref, rows_ref, sems = refs[nodes + 2 :]
    me = lax.axis_index("fsdp")
    capacity = blocks[0].shape[0]
    weight = (
        0.5 * (own_ref[...].astype(jnp.float32) + partner_ref[...].astype(jnp.float32))
    ).astype(jnp.bfloat16)
    weight_ref[...] = weight
    copies = [pltpu.make_async_copy(weight_ref, weight_out, sems.at[nodes])]
    copies[0].start()
    for k in range(nodes):
        slot_ref[k * capacity : (k + 1) * capacity, :] = blocks[k][...]
    rows_ref[...] = (dot_t(slot_ref[...], weight) * (1.0 / math.sqrt(width))).astype(jnp.bfloat16)
    for k in range(nodes):
        home = pl.ds(pl.multiple_of(at(come[k], me) * capacity, capacity), capacity)
        copies.append(
            pltpu.make_async_copy(
                rows_ref.at[k * capacity : (k + 1) * capacity], rows_out.at[home], sems.at[k]
            )
        )
        copies[-1].start()
    turned_ref[...] = weight.T
    for cp in copies:
        cp.wait()


def part_kernel(block_ref, turned_ref, part_ref):
    part_ref[...] = dot(block_ref[...], turned_ref[: block_ref.shape[1], :])


def last_kernel(come, width, block_ref, turned_ref, part_ref, _, rows_out, rows_ref, sem):
    me = lax.axis_index("fsdp")
    capacity = block_ref.shape[0]
    total = part_ref[...] + dot(
        block_ref[...], turned_ref[turned_ref.shape[0] - block_ref.shape[1] :, :]
    )
    rows_ref[...] = (total * (1.0 / math.sqrt(width))).astype(jnp.bfloat16)
    home = pl.ds(pl.multiple_of(at(come, me) * capacity, capacity), capacity)
    cp = pltpu.make_async_copy(rows_ref, rows_out.at[home], sem)
    cp.start()
    cp.wait()


def per_device(momentum, weights, tokens, routes):
    nodes = lax.axis_size("fsdp")
    rows, width = momentum.shape[2], momentum.shape[3]
    total = weights.shape[2]
    tok_rows = tokens.shape[1]
    capacity = 2 * tok_rows // nodes
    here = (tuple(range(nodes)),) * 2
    far = [here, *zip(*(steps(nodes, order) for order in MH))]
    near = [here, *zip(*(steps(nodes, order) for order in TH))]

    source = pltpu.with_memory_space_constraint(momentum[0], pltpu.HBM)
    blocks = []
    for k, step in enumerate(far):
        shard = pl.pallas_call(
            functools.partial(slice_kernel, step),
            out_shape=jax.ShapeDtypeStruct((rows, width), jnp.bfloat16),
            in_specs=[pl.BlockSpec(memory_space=pltpu.HBM)],
            out_specs=VMEM,
            scratch_shapes=[pltpu.SemaphoreType.DMA],
            compiler_params=pltpu.CompilerParams(vmem_limit_bytes=8 << 20),
            name="slice",
        )(source)
        blocks.append(trade(shard, step) if k else shard)

    cut = width // 2
    packed = list(
        pl.pallas_call(
            functools.partial(pack_kernel, near, capacity),
            out_shape=[
                jax.ShapeDtypeStruct((capacity, columns), jnp.bfloat16)
                for columns in (*[width] * (nodes - 1), cut, width - cut)
            ],
            in_specs=[VMEM, VMEM],
            out_specs=[VMEM] * (nodes + 1),
            compiler_params=pltpu.CompilerParams(vmem_limit_bytes=16 << 20),
            cost_estimate=pl.CostEstimate(
                flops=2 * nodes * capacity * tok_rows * width,
                bytes_accessed=2 * (tok_rows + nodes * capacity) * width,
                transcendentals=0,
            ),
            name="pack",
        )(routes.reshape(1, tok_rows), tokens[0])
    )
    slots = [packed[0]]
    for k, step in enumerate([*near[1:], near[-1]], 1):
        slots.append(trade(packed[k], step))

    updated = pl.pallas_call(
        functools.partial(update_kernel, [inverse(s) for s in far], width),
        out_shape=jax.ShapeDtypeStruct((total, width), jnp.bfloat16),
        in_specs=[VMEM] * (nodes + 1),
        out_specs=VMEM,
        scratch_shapes=[pltpu.VMEM((total, width), jnp.bfloat16)],
        compiler_params=pltpu.CompilerParams(vmem_limit_bytes=24 << 20),
        cost_estimate=pl.CostEstimate(
            flops=4 * total * total * width + 10 * total**3,
            bytes_accessed=6 * total * width,
            transcendentals=0,
        ),
        name="update",
    )(*blocks, weights[0, 0])
    partner = lax.ppermute(
        updated, "replica", [(i, i ^ 1 << GOSSIP_BIT) for i in range(lax.axis_size("replica"))]
    )
    come = [inverse(step) for step in near]
    early = nodes - 1
    rows_shape = jax.ShapeDtypeStruct((nodes * capacity, total), jnp.bfloat16)
    hbm = pl.BlockSpec(memory_space=pltpu.HBM)
    averaged, expert_rows, turned = pl.pallas_call(
        functools.partial(project_kernel, come[:early], width),
        out_shape=(
            jax.ShapeDtypeStruct((total, width), jnp.bfloat16),
            rows_shape,
            jax.ShapeDtypeStruct((width, total), jnp.bfloat16),
        ),
        in_specs=[VMEM] * (early + 2),
        out_specs=(hbm, hbm, VMEM),
        scratch_shapes=[
            pltpu.VMEM((total, width), jnp.bfloat16),
            pltpu.VMEM((early * capacity, width), jnp.bfloat16),
            pltpu.VMEM((early * capacity, total), jnp.bfloat16),
            pltpu.SemaphoreType.DMA((nodes,)),
        ],
        compiler_params=pltpu.CompilerParams(vmem_limit_bytes=24 << 20),
        cost_estimate=pl.CostEstimate(
            flops=2 * early * capacity * width * total,
            bytes_accessed=6 * total * width + 2 * early * capacity * (width + total),
            transcendentals=0,
        ),
        name="project",
    )(*slots[:early], updated, partner)
    part = pl.pallas_call(
        part_kernel,
        out_shape=jax.ShapeDtypeStruct((capacity, total), jnp.float32),
        in_specs=[VMEM, VMEM],
        out_specs=VMEM,
        compiler_params=pltpu.CompilerParams(vmem_limit_bytes=24 << 20),
        cost_estimate=pl.CostEstimate(
            flops=2 * capacity * cut * total,
            bytes_accessed=2 * cut * (capacity + total),
            transcendentals=0,
        ),
        name="part",
    )(slots[early], turned)
    expert_rows = pl.pallas_call(
        functools.partial(last_kernel, come[early], width),
        out_shape=rows_shape,
        in_specs=[VMEM, VMEM, VMEM, hbm],
        out_specs=hbm,
        scratch_shapes=[
            pltpu.VMEM((capacity, total), jnp.bfloat16),
            pltpu.SemaphoreType.DMA,
        ],
        input_output_aliases={3: 0},
        compiler_params=pltpu.CompilerParams(vmem_limit_bytes=24 << 20),
        cost_estimate=pl.CostEstimate(
            flops=2 * capacity * width * total,
            bytes_accessed=2 * capacity * (width + total),
            transcendentals=0,
        ),
        name="last",
    )(slots[early + 1], turned, part, expert_rows)
    return (averaged[None, None], expert_rows[None, None])


def solution(mesh):
    in_specs = (
        P("replica", None, "fsdp", None),
        P("replica", "fsdp", None, None),
        P("replica", "fsdp", None),
        P("replica", "fsdp", None),
    )
    out_specs = (P("replica", "fsdp", None, None), P("replica", "fsdp", None, None))

    return jax.shard_map(per_device, mesh=mesh, in_specs=in_specs, out_specs=out_specs, check_vma=False)
```

```python
import functools
import math

import jax
import jax.numpy as jnp
from jax import lax
from jax.experimental import pallas as pl
from jax.experimental.pallas import tpu as pltpu
from jax.sharding import PartitionSpec as P


ITERS = 2
GOSSIP_BIT = 2


coef_a = 3.4445
coef_b = -4.775
coef_c = 2.0315
step_rate = 0.5
MH = (("b3", "b1", 3), ("c3", 1, "c1"))
TH = ((1, "c3", "c1"), (1, "c3", "c1"))
STEPS = {
    1: (1, 0, 3, 2),
    2: (2, 3, 0, 1),
    3: (3, 2, 1, 0),
    "a1": (1, 2, 3, 0),
    "a3": (3, 0, 1, 2),
    "b1": (1, 3, 0, 2),
    "b3": (2, 0, 3, 1),
    "c1": (2, 3, 1, 0),
    "c3": (3, 2, 0, 1),
}

VMEM = pl.BlockSpec(memory_space=pltpu.VMEM)


def dot(a, b):
    return jnp.dot(a, b, preferred_element_type=jnp.float32)


def dot_t(a, b):
    return lax.dot_general(a, b, (((1,), (1,)), ((), ())), preferred_element_type=jnp.float32)


def steps(nodes, order):
    if nodes == 4:
        return [STEPS[k] for k in order]
    if nodes & (nodes - 1) == 0:
        return [tuple(i ^ k for i in range(nodes)) for k in (*range(2, nodes), 1)]
    return [tuple((i + k) % nodes for i in range(nodes)) for k in (*range(2, nodes), 1)]


def inverse(pair):
    return tuple(tuple(step.index(i) for i in range(len(step))) for step in pair)


def entry(step, me):
    hop = step[0]
    if all(to == i ^ hop for i, to in enumerate(step)):
        return me ^ hop
    found = step[0]
    for i, to in enumerate(step[1:], 1):
        found = jnp.where(me == i, to, found)
    return found


def at(pair, me):
    even, odd = pair
    if even == odd:
        return entry(even, me)
    return jnp.where(lax.axis_index("replica") % 2 == 0, entry(even, me), entry(odd, me))


def trade(block, pair):
    nodes = len(pair[0])
    pairs = [
        (r * nodes + i, r * nodes + to)
        for r in range(lax.axis_size("replica"))
        for i, to in enumerate(pair[r % 2])
    ]
    return lax.ppermute(block, ("replica", "fsdp"), pairs)


def slice_kernel(step, source_ref, out_ref, sem):
    cp = pltpu.make_async_copy(source_ref.at[at(step, lax.axis_index("fsdp"))], out_ref, sem)
    cp.start()
    cp.wait()


def pack_kernel(to, capacity, routes_ref, tokens_ref, *out_refs):
    tok_rows = routes_ref.shape[1]
    routes = routes_ref[...]
    me = lax.axis_index("fsdp")
    earlier = lax.broadcasted_iota(jnp.int32, (tok_rows, tok_rows), 0) < lax.broadcasted_iota(
        jnp.int32, (tok_rows, tok_rows), 1
    )
    earlier = jnp.where(earlier, 1.0, 0.0).astype(jnp.bfloat16)
    slot = lax.broadcasted_iota(jnp.int32, (capacity, tok_rows), 0)
    tokens = tokens_ref[...]
    for k, step in enumerate(to):
        here = routes == at(step, me)
        count = dot(jnp.where(here, 1.0, 0.0).astype(jnp.bfloat16), earlier)
        position = jnp.where(here, count.astype(jnp.int32), -1)
        placing = jnp.where(slot == position, 1.0, 0.0).astype(jnp.bfloat16)
        block = dot(placing, tokens).astype(jnp.bfloat16)
        if k + 1 < len(to):
            out_refs[k][...] = block
        else:
            cut = out_refs[k].shape[1]
            out_refs[k][...] = block[:, :cut]
            out_refs[k + 1][...] = block[:, cut:]


def row_parts(rows):
    part = 128 if rows % 128 == 0 else rows
    return [slice(i, i + part) for i in range(0, rows, part)]


def update_kernel(come, width, *refs):
    nodes = len(come)
    blocks, weight_ref, out_ref, x_ref = refs[:nodes], refs[nodes], refs[nodes + 1], refs[nodes + 2]
    me = lax.axis_index("fsdp")
    rows = blocks[0].shape[0]
    total = nodes * rows
    for k in range(nodes):
        x_ref[k * rows : (k + 1) * rows, :] = blocks[k][...]
    x = x_ref[...]
    gram = dot_t(x, x)
    on_diagonal = lax.broadcasted_iota(jnp.int32, (total, total), 0) == lax.broadcasted_iota(
        jnp.int32, (total, total), 1
    )
    square = jnp.sum(jnp.where(on_diagonal, gram, 0.0))
    scale = 1.0 / (jnp.sqrt(jnp.full((1, 1), square, jnp.float32)) + 1e-07)
    gram = gram * scale * scale
    parts = row_parts(total)
    now = [gram[r] for r in parts]
    ortho = x
    for step in range(ITERS):
        low = [g.astype(jnp.bfloat16) for g in now]
        whole = jnp.concatenate(low, 0)
        poly = [coef_b * g + coef_c * dot(h, whole) for g, h in zip(now, low)]
        poly_low = [p.astype(jnp.bfloat16) for p in poly]
        poly_whole = jnp.concatenate(poly_low, 0)
        if step + 1 < ITERS:
            half = [coef_a * g + dot(p, whole) for g, p in zip(now, poly_low)]
            now = [coef_a * h + dot(h.astype(jnp.bfloat16), poly_whole) for h in half]
            ortho = (coef_a * ortho.astype(jnp.float32) + dot(poly_whole, ortho)).astype(jnp.bfloat16)
    rate = step_rate * math.sqrt(width)
    for k in range(nodes):
        r = slice(k * rows, (k + 1) * rows)
        change = dot(poly_whole[r], ortho) + coef_a * ortho[r].astype(jnp.float32)
        home = pl.ds(pl.multiple_of(at(come[k], me) * rows, rows), rows)
        out_ref[home, :] = (
            weight_ref[home, :].astype(jnp.float32) - (rate * scale) * change
        ).astype(jnp.bfloat16)


def project_kernel(nodes, width, *refs):
    blocks, own_ref, partner_ref = refs[:nodes], *refs[nodes : nodes + 2]
    weight_out, rows_ref, turned_ref, weight_ref, slot_ref, sem = refs[nodes + 2 :]
    capacity = blocks[0].shape[0]
    weight = (
        0.5 * (own_ref[...].astype(jnp.float32) + partner_ref[...].astype(jnp.float32))
    ).astype(jnp.bfloat16)
    weight_ref[...] = weight
    cp = pltpu.make_async_copy(weight_ref, weight_out, sem)
    cp.start()
    for k in range(nodes):
        slot_ref[k * capacity : (k + 1) * capacity, :] = blocks[k][...]
    rows_ref[...] = (dot_t(slot_ref[...], weight) * (1.0 / math.sqrt(width))).astype(jnp.bfloat16)
    turned_ref[...] = weight.T
    cp.wait()


def part_kernel(block_ref, turned_ref, part_ref):
    part_ref[...] = dot(block_ref[...], turned_ref[: block_ref.shape[1], :])


def last_kernel(come, width, block_ref, turned_ref, part_ref, held_ref, rows_out, rows_ref, sems):
    me = lax.axis_index("fsdp")
    capacity = block_ref.shape[0]
    early = len(come) - 1

    def put(source, k):
        home = pl.ds(pl.multiple_of(at(come[k], me) * capacity, capacity), capacity)
        cp = pltpu.make_async_copy(source, rows_out.at[home], sems.at[k])
        cp.start()
        return cp

    copies = [put(held_ref.at[k * capacity : (k + 1) * capacity], k) for k in range(early)]
    total = part_ref[...] + dot(
        block_ref[...], turned_ref[turned_ref.shape[0] - block_ref.shape[1] :, :]
    )
    rows_ref[...] = (total * (1.0 / math.sqrt(width))).astype(jnp.bfloat16)
    copies.append(put(rows_ref, early))
    for cp in copies:
        cp.wait()


def per_device(momentum, weights, tokens, routes):
    nodes = lax.axis_size("fsdp")
    rows, width = momentum.shape[2], momentum.shape[3]
    total = weights.shape[2]
    tok_rows = tokens.shape[1]
    capacity = 2 * tok_rows // nodes
    here = (tuple(range(nodes)),) * 2
    far = [here, *zip(*(steps(nodes, order) for order in MH))]
    near = [here, *zip(*(steps(nodes, order) for order in TH))]

    source = pltpu.with_memory_space_constraint(momentum[0], pltpu.HBM)
    blocks = []
    for k, step in enumerate(far):
        shard = pl.pallas_call(
            functools.partial(slice_kernel, step),
            out_shape=jax.ShapeDtypeStruct((rows, width), jnp.bfloat16),
            in_specs=[pl.BlockSpec(memory_space=pltpu.HBM)],
            out_specs=VMEM,
            scratch_shapes=[pltpu.SemaphoreType.DMA],
            compiler_params=pltpu.CompilerParams(vmem_limit_bytes=8 << 20),
            name="slice",
        )(source)
        blocks.append(trade(shard, step) if k else shard)

    cut = width // 2
    packed = list(
        pl.pallas_call(
            functools.partial(pack_kernel, near, capacity),
            out_shape=[
                jax.ShapeDtypeStruct((capacity, columns), jnp.bfloat16)
                for columns in (*[width] * (nodes - 1), cut, width - cut)
            ],
            in_specs=[VMEM, VMEM],
            out_specs=[VMEM] * (nodes + 1),
            compiler_params=pltpu.CompilerParams(vmem_limit_bytes=16 << 20),
            cost_estimate=pl.CostEstimate(
                flops=2 * nodes * capacity * tok_rows * width,
                bytes_accessed=2 * (tok_rows + nodes * capacity) * width,
                transcendentals=0,
            ),
            name="pack",
        )(routes.reshape(1, tok_rows), tokens[0])
    )
    slots = [packed[0]]
    for k, step in enumerate([*near[1:], near[-1]], 1):
        slots.append(trade(packed[k], step))

    updated = pl.pallas_call(
        functools.partial(update_kernel, [inverse(s) for s in far], width),
        out_shape=jax.ShapeDtypeStruct((total, width), jnp.bfloat16),
        in_specs=[VMEM] * (nodes + 1),
        out_specs=VMEM,
        scratch_shapes=[pltpu.VMEM((total, width), jnp.bfloat16)],
        compiler_params=pltpu.CompilerParams(vmem_limit_bytes=24 << 20),
        cost_estimate=pl.CostEstimate(
            flops=4 * total * total * width + 10 * total**3,
            bytes_accessed=6 * total * width,
            transcendentals=0,
        ),
        name="update",
    )(*blocks, weights[0, 0])
    partner = lax.ppermute(
        updated, "replica", [(i, i ^ 1 << GOSSIP_BIT) for i in range(lax.axis_size("replica"))]
    )
    come = [inverse(step) for step in near]
    early = nodes - 1
    rows_shape = jax.ShapeDtypeStruct((nodes * capacity, total), jnp.bfloat16)
    hbm = pl.BlockSpec(memory_space=pltpu.HBM)
    averaged, held_rows, turned = pl.pallas_call(
        functools.partial(project_kernel, early, width),
        out_shape=(
            jax.ShapeDtypeStruct((total, width), jnp.bfloat16),
            jax.ShapeDtypeStruct((early * capacity, total), jnp.bfloat16),
            jax.ShapeDtypeStruct((width, total), jnp.bfloat16),
        ),
        in_specs=[VMEM] * (early + 2),
        out_specs=(hbm, VMEM, VMEM),
        scratch_shapes=[
            pltpu.VMEM((total, width), jnp.bfloat16),
            pltpu.VMEM((early * capacity, width), jnp.bfloat16),
            pltpu.SemaphoreType.DMA,
        ],
        compiler_params=pltpu.CompilerParams(vmem_limit_bytes=24 << 20),
        cost_estimate=pl.CostEstimate(
            flops=2 * early * capacity * width * total,
            bytes_accessed=6 * total * width + 2 * early * capacity * (width + total),
            transcendentals=0,
        ),
        name="project",
    )(*slots[:early], updated, partner)
    part = pl.pallas_call(
        part_kernel,
        out_shape=jax.ShapeDtypeStruct((capacity, total), jnp.float32),
        in_specs=[VMEM, VMEM],
        out_specs=VMEM,
        compiler_params=pltpu.CompilerParams(vmem_limit_bytes=24 << 20),
        cost_estimate=pl.CostEstimate(
            flops=2 * capacity * cut * total,
            bytes_accessed=2 * cut * (capacity + total),
            transcendentals=0,
        ),
        name="part",
    )(slots[early], turned)
    expert_rows = pl.pallas_call(
        functools.partial(last_kernel, come, width),
        out_shape=rows_shape,
        in_specs=[VMEM] * 4,
        out_specs=hbm,
        scratch_shapes=[
            pltpu.VMEM((capacity, total), jnp.bfloat16),
            pltpu.SemaphoreType.DMA((nodes,)),
        ],
        compiler_params=pltpu.CompilerParams(vmem_limit_bytes=24 << 20),
        cost_estimate=pl.CostEstimate(
            flops=2 * capacity * width * total,
            bytes_accessed=2 * capacity * (width + total),
            transcendentals=0,
        ),
        name="last",
    )(slots[early + 1], turned, part, held_rows)
    return (averaged[None, None], expert_rows[None, None])


def solution(mesh):
    in_specs = (
        P("replica", None, "fsdp", None),
        P("replica", "fsdp", None, None),
        P("replica", "fsdp", None),
        P("replica", "fsdp", None),
    )
    out_specs = (P("replica", "fsdp", None, None), P("replica", "fsdp", None, None))

    return jax.shard_map(per_device, mesh=mesh, in_specs=in_specs, out_specs=out_specs, check_vma=False)
```
